32 devices in a mesh: shot: 16 (over z, y, core), surf: 2 (over x).
Axes of the slice: x: 2, y: 2, z: 4, core: 2. Of those that a mesh axis runs over, the one named last changes fastest.
Arguments:
- data: float32 [32, 256, 512], P('shot', 'surf'), may hold values from -6 to 6
- positions: int32 [256], P('surf'), may hold values from 0 to 63, as said below
- plan: int32 [16], replicated, may hold values from 0 to 15, each once
- primaries: bfloat16 [64, 16, 16, 256], P('surf', None, 'shot'), may hold values from -0.03125 to 0.03125
- scale: float32 [32], P('shot'), may hold values from 0.5 to 1.5
Outputs:
- demultiplied: float32 [32, 256, 512], P('shot', 'surf')
The draws below stay inside these ranges and needn't reach their ends.
Inputs may be any that keep to these rules, and one draw needn't show every extreme that they name: `positions`: receiver r lies at a position of the block [b * 32, (b + 1) * 32) with b = r // 128; in each such block of receivers the first maps to the block's first position and the last to its last. A permutation: slot i of primaries holds receiver panel plan[i].
All inputs are finite; a program needn't handle non-finite values.
Results may differ from the reference program's by a relative error of at most 0.0065.
Values may be sent and summed in bfloat16 or wider, within the bound.
A program may use at most 128 MiB of HBM per device.

```python
import math
import jax
import jax.numpy as jnp
from jax import lax

S_DEV = 2
PD = 32
RP = 16
NT = 512
TAPS = 256
PANELS = 16
SHOTS = 32
RECV = 256
RECV_DEV = 128
POSITIONS = 64
N_SURF = 2


def draw_positions(key, part):
    receiver_index = jnp.arange(RECV, dtype=jnp.int32)
    offset = receiver_index % RECV_DEV
    block_index = receiver_index // RECV_DEV
    picked = jax.random.randint(key, (RECV,), 0, PD, dtype=jnp.int32)
    picked = jnp.where(offset == 0, 0, jnp.where(offset == RECV_DEV - 1, PD - 1, picked))
    return (block_index * PD + picked).astype(jnp.int32)


def levels(rng, shape, cuts, smallest, top_value):
    def one(axis_at, blocks):
        heights = jax.random.uniform(jax.random.fold_in(jax.random.fold_in(rng, 6), axis_at), (blocks,), jnp.float32, smallest / len(cuts), top_value / len(cuts))
        return jnp.repeat(jnp.exp(heights), shape[axis_at] // blocks).reshape((-1,) + (1,) * (len(shape) - axis_at - 1))

    gain = one(*cuts[0])
    for cut in cuts[1:]:
        gain = gain * one(*cut)
    return gain


def centred(rng, dims, width, limit, pieces=(), held_as=jnp.bfloat16):
    loudness = levels(rng, dims, pieces, -0.22, 0.18) if pieces else 1.0
    drawn = jax.random.normal(rng, dims, jnp.float32) * width * loudness
    return jnp.minimum(jnp.maximum(drawn, -limit), limit).astype(held_as)


def setup_inputs(seed: int = 0) -> dict:
    arg_keys = jax.random.split(jax.random.key(seed), 6)
    return {
        "data": centred(arg_keys[0], (SHOTS, RECV, NT), 1.0, 6.0, ((0, 16), (1, 2)), jnp.float32),
        "positions": draw_positions(jax.random.fold_in(arg_keys[5], 71), 0),
        "plan": jax.random.permutation(arg_keys[2], PANELS).astype(jnp.int32),
        "primaries": centred(arg_keys[3], (POSITIONS, RP, PANELS, TAPS), (2 * POSITIONS * TAPS) ** -0.5, 0.03125, ((0, 2), (2, 16))),
        "scale": jnp.clip(jnp.exp(math.log(1.5) - 1.0986123 * jax.random.uniform(arg_keys[4], (SHOTS,), jnp.float32) ** levels(arg_keys[4], (SHOTS,), ((0, 16),), -0.2, 0.2)), 0.5, 1.5),
    }


def fourier_matrices(samples):
    length = 2 * samples
    time_index = jnp.arange(samples, dtype=jnp.int32)
    phase_index = (time_index[:, None] * time_index[None, :]) % length
    angles = phase_index.astype(jnp.float32) * (2.0 * math.pi / length)
    cosine = jnp.cos(angles)
    sine_part = jnp.sin(angles)
    alternate = (1 - 2 * (time_index % 2)).astype(jnp.float32)
    nyquist = time_index == 0
    forward_imag = jnp.where(nyquist[None, :], alternate[:, None], -sine_part)
    forward = jnp.concatenate([cosine, forward_imag], axis=1).astype(jnp.bfloat16)
    weights = jnp.where(nyquist, 1.0, 2.0).astype(jnp.float32) / length
    backward_real_table = cosine.T * weights[:, None]
    inverse_imag = jnp.where(nyquist[:, None], alternate[None, :] / length, -2.0 * sine_part.T / length)
    inverse = jnp.concatenate([backward_real_table, inverse_imag], axis=0).astype(jnp.bfloat16)
    return forward, inverse


def spectral_product(left, right):
    half = left.shape[-1] // 2
    left_real = left[..., :half]
    left_imag = left[..., half:]
    right_real = right[..., :half]
    right_imag = right[..., half:]

    def contract(leading_factor, trailing_factor):
        return jnp.einsum("quw,ugw->qgw", leading_factor, trailing_factor, precision=lax.Precision.HIGHEST)

    real_cross_term = contract(left_real, right_real)
    imaginary_cross_term = contract(left_imag, right_imag)
    crossed = contract(left_real, right_imag) + contract(left_imag, right_real)
    interior = (jnp.arange(half) > 0).astype(jnp.float32)
    return jnp.concatenate([real_cross_term - interior * imaginary_cross_term, interior * crossed + (1.0 - interior) * imaginary_cross_term], axis=-1)


def reference(data, positions, plan, primaries, scale):
    shot_total, receiver_total, samples = data.shape
    position_total = primaries.shape[0]
    tap_count = primaries.shape[3]
    forward, inverse = fourier_matrices(samples)
    onehot = (positions[:, None] == jnp.arange(position_total, dtype=jnp.int32)[None, :]).astype(jnp.float32)
    gathered = jnp.einsum("srt,rx->sxt", data, onehot, precision=lax.Precision.HIGHEST).astype(jnp.bfloat16)
    data_spectra = jnp.dot(gathered.reshape(-1, samples), forward, preferred_element_type=jnp.float32)
    data_spectra = data_spectra.astype(jnp.bfloat16).reshape(shot_total, position_total, 2 * samples)
    panel_order = jnp.argsort(plan).astype(jnp.int32)
    arranged = jnp.take(primaries, panel_order, axis=2)
    primary_spectra = jnp.dot(arranged.reshape(-1, tap_count), forward[:tap_count], preferred_element_type=jnp.float32)
    primary_spectra = primary_spectra.astype(jnp.bfloat16).astype(jnp.float32).reshape(position_total, receiver_total, 2 * samples)

    def one_group(group_spectra):
        group_wide = group_spectra.astype(jnp.float32)
        running = jnp.zeros((group_spectra.shape[0], receiver_total, 2 * samples), jnp.float32)
        for block_index in range(N_SURF):
            low = block_index * PD
            term = spectral_product(group_wide[:, low:low + PD], primary_spectra[low:low + PD])
            rounded = lax.optimization_barrier(term.astype(jnp.bfloat16))
            running = running + rounded.astype(jnp.float32)
        spectrum = running.astype(jnp.bfloat16)
        in_time = jnp.dot(spectrum.reshape(-1, 2 * samples), inverse, preferred_element_type=jnp.float32)
        return in_time.reshape(group_spectra.shape[0], receiver_total, samples)

    grouped = data_spectra.reshape(shot_total // S_DEV, S_DEV, position_total, 2 * samples)
    prediction = lax.map(one_group, grouped).reshape(shot_total, receiver_total, samples)
    return data - scale[:, None, None] * prediction
```

```python
import functools
import math

import jax
import jax.numpy as jnp
import ml_dtypes
import numpy as np
from jax import lax
from jax.experimental import pallas as pl
from jax.experimental.pallas import tpu as pltpu
from jax.sharding import PartitionSpec as P

MESH = pl.DeviceIdType.MESH
F32 = jnp.float32
BF16 = jnp.bfloat16
UNROLL = 16
LAG = 2
BLOCK = 8


def fourier_matrices(samples, length):
    half = length // 2
    time, frequency = np.arange(samples), np.arange(half)
    angles = (time[:, None] * frequency[None, :] % length) * (2.0 * math.pi / length)
    cosine, sine = np.cos(angles), np.sin(angles)
    forward_imag = -sine
    forward_imag[:, 0] = 1.0 - 2.0 * (time % 2)
    forward = np.concatenate([cosine, forward_imag], axis=1)
    weights = np.where(frequency == 0, 1.0, 2.0) / length
    weights = np.concatenate([weights, weights])
    inverse = forward.T * weights[:, None]
    return forward.astype(ml_dtypes.bfloat16), inverse.astype(ml_dtypes.bfloat16)


def predict_kernel(
    sizes,
    positions_hbm, data_hbm, primaries_hbm, forward_hbm, inverse_hbm,
    out_hbm,
    positions_ref, data_ref, forward_ref, inverse_ref, panels, gathered, e1, e2, e3, factors, spectrum,
    crossing, crossed, leaving,
    load_sems, data_sems, mate_sems, y_send, y_recv, relay_send, relay_recv, g_send, g_recv,
    cross_send, cross_recv, leave_send, leave_recv, own_sems,
):
    heights, surfs, shots, depth, width, samples, taps, half = sizes
    per_surf = width // surfs
    pieces = depth // BLOCK
    piece_rows = BLOCK * width
    items = 2 * heights
    tiles_f = half // 128
    shot = lax.axis_index("shot")
    surf = lax.axis_index("surf")
    core = shot % 2
    side = shot // 2 % 2
    height = shot // 4
    mate = (height * 2 + side) * 2 + 1 - core
    across = (height * 2 + 1 - side) * 2 + core

    def line(z):
        return (z * 2 + side) * 2 + core

    barrier = pltpu.get_barrier_semaphore()
    for to in (across, mate):
        pl.semaphore_signal(barrier, inc=1, device_id=(to, surf), device_id_type=MESH)
    for z in range(heights):

        @pl.when(z != height)
        def _():
            pl.semaphore_signal(barrier, inc=1, device_id=(line(z), surf), device_id_type=MESH)

    for h in range(surfs):

        @pl.when(h != surf)
        def _():
            pl.semaphore_signal(barrier, inc=1, device_id=(shot, h), device_id_type=MESH)

    load_positions = pltpu.make_async_copy(positions_hbm, positions_ref, load_sems.at[0])
    load_positions.start()
    load_data = [pltpu.make_async_copy(data_hbm.at[s], data_ref.at[s], data_sems.at[s]) for s in range(shots)]
    for load in load_data:
        load.start()
    load_panel = pltpu.make_async_copy(primaries_hbm, panels.at[0], load_sems.at[1])
    load_forward = pltpu.make_async_copy(forward_hbm, forward_ref, load_sems.at[2])
    load_inverse = pltpu.make_async_copy(inverse_hbm, inverse_ref, load_sems.at[3])
    load_panel.start()
    load_forward.start()
    load_inverse.start()

    pl.semaphore_wait(barrier, heights + surfs)

    mate_copy = pltpu.make_async_remote_copy(
        src_ref=primaries_hbm,
        dst_ref=panels.at[1],
        send_sem=mate_sems.at[0],
        recv_sem=mate_sems.at[1],
        device_id=(mate, surf),
        device_id_type=MESH,
    )

    def rows_of(n):
        return pl.ds(pl.multiple_of(n * piece_rows, piece_rows), piece_rows)

    def y_copy(n):
        return pltpu.make_async_remote_copy(
            src_ref=primaries_hbm.at[rows_of(n)],
            dst_ref=panels.at[2, rows_of(n)],
            send_sem=y_send.at[n],
            recv_sem=y_recv.at[n],
            device_id=(across, surf),
            device_id_type=MESH,
        )

    def relay_copy(n):
        return pltpu.make_async_remote_copy(
            src_ref=panels.at[2, rows_of(n)],
            dst_ref=panels.at[3, rows_of(n)],
            send_sem=relay_send.at[n],
            recv_sem=relay_recv.at[n],
            device_id=(mate, surf),
            device_id_type=MESH,
        )

    for n in range(pieces):
        y_copy(n).start()
    mate_copy.start()

    load_positions.wait()
    local = positions_ref[...] - surf * depth
    onehot = jnp.where(
        lax.broadcasted_iota(jnp.int32, (depth, local.shape[1]), 0) == local, 1.0, 0.0
    ).astype(BF16)
    for s in range(shots):
        load_data[s].wait()
        value = data_ref[s]
        top = value.astype(BF16)
        rest = value - top.astype(F32)
        middle = rest.astype(BF16)
        low = (rest - middle.astype(F32)).astype(BF16)
        total = (
            jnp.dot(onehot, top, preferred_element_type=F32)
            + jnp.dot(onehot, middle, preferred_element_type=F32)
            + jnp.dot(onehot, low, preferred_element_type=F32)
        )
        gathered[height, s * depth:(s + 1) * depth, :] = total.astype(BF16)

    def order(k):
        upper = height // (heights // 2)
        toward = 1 - 2 * upper
        short = height + upper * (heights - 1 - 2 * height)
        past = (k - 2 * short - 1 + 4 * heights) // (4 * heights)
        near = (k + 1) // 2 * (2 * (k % 2) - 1)
        return height + toward * (past * (k - short) + (1 - past) * near)

    def g_copy(z):
        return pltpu.make_async_remote_copy(
            src_ref=gathered.at[height],
            dst_ref=gathered.at[height],
            send_sem=g_send.at[z],
            recv_sem=g_recv.at[height],
            device_id=(line(z), surf),
            device_id_type=MESH,
        )

    for k in range(1, heights):
        g_copy(order(k)).start()

    def panel_spectra(which, pair, lane, n):
        rows = panels[which, rows_of(n), :]
        value = jnp.dot(rows, forward_ref[:taps, :], preferred_element_type=F32)
        real, imag = value[:, :half], value[:, half:]
        first = lax.broadcasted_iota(jnp.int32, real.shape, 1) == 0
        at = pl.ds(pl.multiple_of(n * BLOCK, BLOCK), BLOCK)
        values = (
            jnp.where(first, 0.0, real),
            jnp.where(first, real, imag - real),
            jnp.where(first, imag, imag + real),
        )
        for ref, value in zip((e1, e2, e3), values):
            for f in range(tiles_f):
                ref[pair, f, at, lane] = value[:, f * 128:(f + 1) * 128].reshape(BLOCK, width, 128)

    def whole_panel(which, pair, lane):
        def step(n, carry):
            panel_spectra(which, pair, lane, n)
            return carry

        lax.fori_loop(0, pieces, step, 0)

    load_forward.wait()
    load_panel.wait()
    whole_panel(0, 0, 0)
    mate_copy.wait_recv()
    whole_panel(1, 0, 1)
    load_inverse.wait()

    def cross_copy(e, to):
        return pltpu.make_async_remote_copy(
            src_ref=crossing.at[e, to],
            dst_ref=crossed.at[e, surf],
            send_sem=cross_send.at[e, to],
            recv_sem=cross_recv.at[e, surf],
            device_id=(shot, to),
            device_id_type=MESH,
        )

    def place_of(e):
        pair = e // heights
        return pair, e + pair * (items - 1 - 2 * e)

    def leave_copy(e):
        pair, k = place_of(e)
        return pltpu.make_async_remote_copy(
            src_ref=leaving.at[e],
            dst_ref=out_hbm.at[height, pair],
            send_sem=leave_send.at[e],
            recv_sem=leave_recv.at[height, pair],
            device_id=(line(order(k)), surf),
            device_id_type=MESH,
        )

    def own_copy(e):
        pair, _ = place_of(e)
        return pltpu.make_async_copy(leaving.at[e], out_hbm.at[height, pair], own_sems.at[pair])

    def pass_on(e):
        for h in range(surfs):

            @pl.when(h != surf)
            def _():
                pltpu.make_async_copy(crossed.at[e, h], crossed.at[e, h], cross_recv.at[e, h]).wait()

        total = crossed[e, 0].astype(F32)
        for h in range(1, surfs):
            total = total + crossed[e, h].astype(F32)
        leaving[e] = total.astype(BF16)
        _, k = place_of(e)

        @pl.when(k != 0)
        def _():
            leave_copy(e).start()

        @pl.when(k == 0)
        def _():
            own_copy(e).start()

    def shot_spectra(k):
        slot = order(k)

        @pl.when(k != 0)
        def _():
            pltpu.make_async_copy(gathered.at[slot], gathered.at[slot], g_recv.at[slot]).wait()

        value = jnp.dot(gathered[slot], forward_ref[...], preferred_element_type=F32)
        real, imag = value[:, :half], value[:, half:]
        for m, part in enumerate((real + imag, real, imag)):
            for s in range(shots):
                for f in range(tiles_f):
                    factors[k, f, s * 3 + m, :depth, :] = part[
                        s * depth:(s + 1) * depth, f * 128:(f + 1) * 128
                    ]

    def work(e, k, pair):
        def one_tile(f, inner):
            lanes = pl.ds(pl.multiple_of(f * 128, 128), 128)
            tiles = 2 * width // 8

            def positions(n, sums):
                sums = list(sums)
                for j in range(UNROLL):
                    x = n * UNROLL + j
                    rows = [
                        [
                            jnp.broadcast_to(
                                factors.at[k, f, s * 3 + m, pl.ds(pl.multiple_of(n * UNROLL, UNROLL), UNROLL)][j:j + 1],
                                (8, 128),
                            )
                            for m in range(3)
                        ]
                        for s in range(shots)
                    ]
                    for t in range(tiles):
                        b, q = t * 8 // width, t * 8 % width
                        for m, ref in enumerate((e1, e2, e3)):
                            factor = ref[pair, f, x, b, q:q + 8]
                            for s in range(shots):
                                at = (s * 3 + m) * tiles + t
                                sums[at] = sums[at] + factor * rows[s][m]
                return tuple(sums)

            zero = jnp.zeros((8, 128), F32)
            sums = lax.fori_loop(
                0, depth // UNROLL, positions, (zero,) * (3 * shots * tiles)
            )
            k1, k2, k3 = [
                [
                    jnp.concatenate(sums[(s * 3 + m) * tiles:(s * 3 + m + 1) * tiles], axis=0)
                    for s in range(shots)
                ]
                for m in range(3)
            ]
            first = lax.broadcasted_iota(jnp.int32, (2 * width, 128), 1) + f * 128 == 0
            imag_lanes = pl.ds(pl.multiple_of(half + f * 128, 128), 128)
            for s in range(shots):
                re = jnp.where(first, k2[s], k1[s] - k3[s])
                im = jnp.where(first, k3[s], k1[s] + k2[s])
                for h in range(surfs):
                    for b in range(2):
                        low = ((h * shots + s) * 2 + b) * per_surf
                        src = b * width + h * per_surf
                        spectrum[low:low + per_surf, lanes] = re[src:src + per_surf]
                        spectrum[low:low + per_surf, imag_lanes] = im[src:src + per_surf]
            return inner

        lax.fori_loop(0, tiles_f, one_tile, 0)
        back = jnp.dot(spectrum[...].astype(BF16), inverse_ref[...], preferred_element_type=F32)
        rows = shots * 2 * per_surf
        for h in range(surfs):
            piece = back[h * rows:(h + 1) * rows].astype(BF16)

            @pl.when(surf == h)
            def _():
                crossed[e, h] = piece

            @pl.when(surf != h)
            def _():
                crossing[e, h] = piece
                cross_copy(e, h).start()

    def take_piece(n):
        pltpu.make_async_copy(panels.at[2, rows_of(n)], panels.at[2, rows_of(n)], y_recv.at[n]).wait()
        relay_copy(n).start()
        panel_spectra(2, 1, 0, n)

    early = min(heights - 1, pieces)

    def first_pair(e, carry):
        @pl.when(e * (early + 1 - e) > 0)
        def _():
            take_piece(e - 1)

        shot_spectra(e)
        work(e, e, 0)

        @pl.when(e >= LAG)
        def _():
            pass_on(e - LAG)

        return carry

    lax.fori_loop(0, heights, first_pair, 0)

    def late_piece(n, carry):
        take_piece(n)
        return carry

    lax.fori_loop(early, pieces, late_piece, 0)

    def relayed_piece(n, carry):
        pltpu.make_async_copy(panels.at[3, rows_of(n)], panels.at[3, rows_of(n)], relay_recv.at[n]).wait()
        panel_spectra(3, 1, 1, n)
        return carry

    lax.fori_loop(0, pieces, relayed_piece, 0)

    def second_pair(e, carry):
        pass_on(e - LAG)
        work(e, items - 1 - e, 1)
        return carry

    lax.fori_loop(heights, items, second_pair, 0)
    for e in range(items - LAG, items):
        pass_on(e)

    def settle(z, carry):
        for pair in range(2):
            at = pair * (items - 1)

            @pl.when(z != height)
            def _():
                pltpu.make_async_copy(out_hbm.at[z, pair], out_hbm.at[z, pair], leave_recv.at[z, pair]).wait()

        @pl.when(z != height)
        def _():
            g_copy(z).wait_send()

        @pl.when(z != 0)
        def _():
            leave_copy(z).wait_send()
            leave_copy(items - 1 - z).wait_send()

        return carry

    lax.fori_loop(0, heights, settle, 0)
    own_copy(0).wait()
    own_copy(items - 1).wait()

    def settle_cross(e, carry):
        for h in range(surfs):

            @pl.when(h != surf)
            def _():
                cross_copy(e, h).wait_send()

        return carry

    lax.fori_loop(0, items, settle_cross, 0)
    for n in range(pieces):
        y_copy(n).wait_send()
        relay_copy(n).wait_send()
    mate_copy.wait_send()


def subtract_kernel(panels, plan_ref, scale_ref, where_ref, data_ref, moved_ref, out_ref):
    shot = lax.axis_index("shot")
    core = shot % 2
    side = shot // 2 % 2
    s = pl.program_id(0)
    line, far, swap, base = [where_ref[n:n + 1, :] for n in range(4)]
    panel = line + 2 * (far + side - 2 * side * far) + swap + core - 2 * core * swap
    target = base
    for n in range(panels):
        target = target + jnp.where(panel == n, plan_ref[n], 0)
    receivers = data_ref.shape[1]
    place_rows = jnp.where(
        lax.broadcasted_iota(jnp.int32, (receivers, target.shape[1]), 0) + s * receivers == target, 1.0, 0.0
    ).astype(BF16)
    prediction = jnp.dot(place_rows, moved_ref[...], preferred_element_type=F32)
    out_ref[0] = data_ref[0] - scale_ref[s] * prediction


def on_device(heights, surfs, data, positions, plan, primaries, scale):
    shots, receivers, samples = data.shape
    depth, width, _, taps = primaries.shape
    per_surf = width // surfs
    half = -(-(samples + taps - 1) // 256) * 128
    forward, inverse = fourier_matrices(samples, 2 * half)
    rows = shots * 2 * per_surf
    items = 2 * heights
    pieces = depth // BLOCK
    panels = 4 * heights
    order = [
        (4 * z, pair, b, s * receivers + q * panels)
        for z in range(heights)
        for pair in range(2)
        for s in range(shots)
        for b in range(2)
        for q in range(per_surf)
    ]
    where_rows = np.zeros((8, len(order)), np.int32)
    where_rows[:4] = np.array(order, np.int32).T
    anywhere = pl.BlockSpec(memory_space=pl.ANY)
    dma = pltpu.SemaphoreType.DMA
    sizes = (heights, surfs, shots, depth, width, samples, taps, half)
    spectra = pltpu.VMEM((2, half // 128, depth, 2, width, 128), F32)
    moved = pl.pallas_call(
        functools.partial(predict_kernel, sizes),
        out_shape=jax.ShapeDtypeStruct((heights, 2, rows, samples), BF16),
        in_specs=[anywhere] * 5,
        out_specs=anywhere,
        scratch_shapes=[
            pltpu.VMEM((1, receivers), jnp.int32),
            pltpu.VMEM(data.shape, F32),
            pltpu.VMEM(forward.shape, BF16),
            pltpu.VMEM(inverse.shape, BF16),
            pltpu.VMEM((4, depth * width, taps), BF16),
            pltpu.VMEM((heights, shots * depth, samples), BF16),
            spectra,
            spectra,
            spectra,
            pltpu.VMEM((heights, half // 128, shots * 3, depth + 8, 128), F32),
            pltpu.VMEM((surfs * rows, 2 * half), F32),
            pltpu.VMEM((items, surfs, rows, samples), BF16),
            pltpu.VMEM((items, surfs, rows, samples), BF16),
            pltpu.VMEM((items, rows, samples), BF16),
            dma((4,)),
            dma((shots,)),
            dma((2,)),
            dma((pieces,)),
            dma((pieces,)),
            dma((pieces,)),
            dma((pieces,)),
            dma((heights,)),
            dma((heights,)),
            dma((items, surfs)),
            dma((items, surfs)),
            dma((items,)),
            dma((heights, 2)),
            dma((2,)),
        ],
        compiler_params=pltpu.CompilerParams(collective_id=0, has_side_effects=True),
        name="predict",
    )(
        positions.reshape(1, receivers),
        data,
        primaries.reshape(depth * width, taps),
        jnp.asarray(forward),
        jnp.asarray(inverse),
    )
    smem = pl.BlockSpec(memory_space=pltpu.SMEM)
    traces = pl.BlockSpec((1, receivers, samples), lambda s: (s, 0, 0))
    return pl.pallas_call(
        functools.partial(subtract_kernel, panels),
        out_shape=jax.ShapeDtypeStruct(data.shape, data.dtype),
        grid=(shots,),
        in_specs=[
            smem,
            smem,
            pl.BlockSpec(where_rows.shape, lambda s: (0, 0)),
            traces,
            pl.BlockSpec((len(order), samples), lambda s: (0, 0)),
        ],
        out_specs=traces,
        name="subtract",
    )(plan, scale, jnp.asarray(where_rows), data, moved.reshape(len(order), samples))


def solution(mesh):
    heights, surfs = mesh.shape["shot"] // 4, mesh.shape["surf"]
    in_specs = (P("shot", "surf", None), P("surf"), P(), P("surf", None, "shot", None), P("shot"))
    out_specs = P("shot", "surf", None)
    return jax.shard_map(
        functools.partial(on_device, heights, surfs),
        mesh=mesh, in_specs=in_specs, out_specs=out_specs, check_vma=False,
    )
```

```python
import functools
import math

import jax
import jax.numpy as jnp
import ml_dtypes
import numpy as np
from jax import lax
from jax.experimental import pallas as pl
from jax.experimental.pallas import tpu as pltpu
from jax.sharding import PartitionSpec as P

MESH = pl.DeviceIdType.MESH
F32 = jnp.float32
BF16 = jnp.bfloat16
UNROLL = 16
BLOCK = 16


def fourier_matrices(samples, length):
    half = length // 2
    time, frequency = np.arange(samples), np.arange(half)
    angles = (time[:, None] * frequency[None, :] % length) * (2.0 * math.pi / length)
    cosine, sine = np.cos(angles), np.sin(angles)
    forward_imag = -sine
    forward_imag[:, 0] = 1.0 - 2.0 * (time % 2)
    forward = np.concatenate([cosine, forward_imag], axis=1)
    weights = np.where(frequency == 0, 1.0, 2.0) / length
    weights = np.concatenate([weights, weights])
    inverse = forward.T * weights[:, None]
    return forward.astype(ml_dtypes.bfloat16), inverse.astype(ml_dtypes.bfloat16)


def predict_kernel(
    sizes,
    plan_hbm, scale_hbm, where_hbm, positions_hbm, data_hbm, primaries_hbm, forward_hbm, inverse_hbm,
    out_ref,
    plan_ref, scale_ref, where_ref, positions_ref, data_ref, forward_ref, inverse_ref,
    panels, gathered, e1, e2, e3, factors, spectrum, leaving, arrived, place_rows, prediction,
    load_sems, data_sems, mate_sems, y_send, y_recv, relay_send, relay_recv, g_send, g_recv,
    leave_send, leave_recv, own_sems,
):
    heights, surfs, shots, depth, width, samples, taps, half = sizes
    per_surf = width // surfs
    pieces = depth // BLOCK
    piece_rows = BLOCK * width
    rows_item = shots * 2 * per_surf
    items = 2 * heights
    tiles_f = half // 128
    shot = lax.axis_index("shot")
    surf = lax.axis_index("surf")
    core = shot % 2
    side = shot // 2 % 2
    height = shot // 4
    mate = (height * 2 + side) * 2 + 1 - core
    across = (height * 2 + 1 - side) * 2 + core

    def line(z):
        return (z * 2 + side) * 2 + core

    barrier = pltpu.get_barrier_semaphore()
    for to in (across, mate):
        pl.semaphore_signal(barrier, inc=1, device_id=(to, surf), device_id_type=MESH)
    for z in range(heights):
        for h in range(surfs):

            @pl.when((z != height) | (h != surf))
            def _():
                pl.semaphore_signal(barrier, inc=1, device_id=(line(z), h), device_id_type=MESH)

    load_positions = pltpu.make_async_copy(positions_hbm, positions_ref, load_sems.at[0])
    load_positions.start()
    load_data = [pltpu.make_async_copy(data_hbm.at[s], data_ref.at[s], data_sems.at[s]) for s in range(shots)]
    for load in load_data:
        load.start()
    load_panel = pltpu.make_async_copy(primaries_hbm, panels.at[0], load_sems.at[1])
    load_forward = pltpu.make_async_copy(forward_hbm, forward_ref, load_sems.at[2])
    load_inverse = pltpu.make_async_copy(inverse_hbm, inverse_ref, load_sems.at[3])
    load_small = [
        pltpu.make_async_copy(src, dst, load_sems.at[4 + n])
        for n, (src, dst) in enumerate(((plan_hbm, plan_ref), (scale_hbm, scale_ref), (where_hbm, where_ref)))
    ]
    mate_copy = pltpu.make_async_remote_copy(
        src_ref=primaries_hbm,
        dst_ref=panels.at[1],
        send_sem=mate_sems.at[0],
        recv_sem=mate_sems.at[1],
        device_id=(mate, surf),
        device_id_type=MESH,
    )

    def rows_of(n):
        return pl.ds(pl.multiple_of(n * piece_rows, piece_rows), piece_rows)

    def y_copy(n):
        return pltpu.make_async_remote_copy(
            src_ref=primaries_hbm.at[rows_of(n)],
            dst_ref=panels.at[2, rows_of(n)],
            send_sem=y_send.at[n],
            recv_sem=y_recv.at[n],
            device_id=(across, surf),
            device_id_type=MESH,
        )

    def relay_copy(n):
        return pltpu.make_async_remote_copy(
            src_ref=panels.at[2, rows_of(n)],
            dst_ref=panels.at[3, rows_of(n)],
            send_sem=relay_send.at[n],
            recv_sem=relay_recv.at[n],
            device_id=(mate, surf),
            device_id_type=MESH,
        )

    load_positions.wait()
    local = positions_ref[...] - surf * depth
    onehot = jnp.where(
        lax.broadcasted_iota(jnp.int32, (depth, local.shape[1]), 0) == local, 1.0, 0.0
    ).astype(BF16)
    for s in range(shots):
        load_data[s].wait()
        if s == shots - 1:
            load_panel.start()
            load_forward.start()
            load_inverse.start()
            for load in load_small:
                load.start()
        value = data_ref[s]
        top = value.astype(BF16)
        rest = value - top.astype(F32)
        middle = rest.astype(BF16)
        low = (rest - middle.astype(F32)).astype(BF16)
        total = (
            jnp.dot(onehot, top, preferred_element_type=F32)
            + jnp.dot(onehot, middle, preferred_element_type=F32)
            + jnp.dot(onehot, low, preferred_element_type=F32)
        )
        gathered[height, s * depth:(s + 1) * depth, :] = total.astype(BF16)

    def order(k):
        upper = height // (heights // 2)
        toward = 1 - 2 * upper
        short = height + upper * (heights - 1 - 2 * height)
        past = (k - 2 * short - 1 + 4 * heights) // (4 * heights)
        near = (k + 1) // 2 * (2 * (k % 2) - 1)
        return height + toward * (past * (k - short) + (1 - past) * near)

    def g_copy(z):
        return pltpu.make_async_remote_copy(
            src_ref=gathered.at[height],
            dst_ref=gathered.at[height],
            send_sem=g_send.at[z],
            recv_sem=g_recv.at[height],
            device_id=(line(z), surf),
            device_id_type=MESH,
        )

    def panel_spectra(which, pair, lane, n, block):
        rows = panels[which, pl.ds(pl.multiple_of(n * block * width, block * width), block * width), :]
        value = jnp.dot(rows, forward_ref[:taps, :], preferred_element_type=F32)
        real, imag = value[:, :half], value[:, half:]
        first = lax.broadcasted_iota(jnp.int32, real.shape, 1) == 0
        at = pl.ds(pl.multiple_of(n * block, block), block)
        values = (
            jnp.where(first, 0.0, real),
            jnp.where(first, real, imag - real),
            jnp.where(first, imag, imag + real),
        )
        for ref, value in zip((e1, e2, e3), values):
            for f in range(tiles_f):
                ref[pair, f, at, lane] = value[:, f * 128:(f + 1) * 128].reshape(block, width, 128)

    def place_of(e):
        pair = e // heights
        return pair, e + pair * (items - 1 - 2 * e)

    def leave_copy(e, h):
        pair, k = place_of(e)
        return pltpu.make_async_remote_copy(
            src_ref=leaving.at[e, h],
            dst_ref=arrived.at[height, pair, surf],
            send_sem=leave_send.at[e, h],
            recv_sem=leave_recv.at[height, pair, surf],
            device_id=(line(order(k)), h),
            device_id_type=MESH,
        )

    def own_copy(pair):
        return pltpu.make_async_copy(
            leaving.at[pair * (items - 1), surf], arrived.at[height, pair, surf], own_sems.at[pair]
        )

    def shot_spectra(k):
        slot = order(k)
        value = jnp.dot(gathered[slot], forward_ref[...], preferred_element_type=F32)
        real, imag = value[:, :half], value[:, half:]
        for m, part in enumerate((real + imag, real, imag)):
            for s in range(shots):
                for f in range(tiles_f):
                    factors[k, f, s * 3 + m, :depth, :] = part[
                        s * depth:(s + 1) * depth, f * 128:(f + 1) * 128
                    ]

    def work(e, k, pair):
        def one_tile(f, inner):
            lanes = pl.ds(pl.multiple_of(f * 128, 128), 128)
            tiles = 2 * width // 8

            def positions(n, sums):
                sums = list(sums)
                for j in range(UNROLL):
                    x = n * UNROLL + j
                    rows = [
                        [
                            jnp.broadcast_to(
                                factors.at[k, f, s * 3 + m, pl.ds(pl.multiple_of(n * UNROLL, UNROLL), UNROLL)][j:j + 1],
                                (8, 128),
                            )
                            for m in range(3)
                        ]
                        for s in range(shots)
                    ]
                    for t in range(tiles):
                        b, q = t * 8 // width, t * 8 % width
                        for m, ref in enumerate((e1, e2, e3)):
                            factor = ref[pair, f, x, b, q:q + 8]
                            for s in range(shots):
                                at = (s * 3 + m) * tiles + t
                                sums[at] = sums[at] + factor * rows[s][m]
                return tuple(sums)

            zero = jnp.zeros((8, 128), F32)
            sums = lax.fori_loop(
                0, depth // UNROLL, positions, (zero,) * (3 * shots * tiles)
            )
            k1, k2, k3 = [
                [
                    jnp.concatenate(sums[(s * 3 + m) * tiles:(s * 3 + m + 1) * tiles], axis=0)
                    for s in range(shots)
                ]
                for m in range(3)
            ]
            first = lax.broadcasted_iota(jnp.int32, (2 * width, 128), 1) + f * 128 == 0
            imag_lanes = pl.ds(pl.multiple_of(half + f * 128, 128), 128)
            for s in range(shots):
                re = jnp.where(first, k2[s], k1[s] - k3[s])
                im = jnp.where(first, k3[s], k1[s] + k2[s])
                for h in range(surfs):
                    for b in range(2):
                        low = ((h * shots + s) * 2 + b) * per_surf
                        src = b * width + h * per_surf
                        spectrum[low:low + per_surf, lanes] = re[src:src + per_surf]
                        spectrum[low:low + per_surf, imag_lanes] = im[src:src + per_surf]
            return inner

        lax.fori_loop(0, tiles_f, one_tile, 0)
        back = jnp.dot(spectrum[...].astype(BF16), inverse_ref[...], preferred_element_type=F32)
        rows = shots * 2 * per_surf
        for h in range(surfs):
            leaving[e, h] = back[h * rows:(h + 1) * rows].astype(BF16)
        for h in range(surfs):

            @pl.when((k != 0) | (h != surf))
            def _():
                leave_copy(e, h).start()

        @pl.when(k == 0)
        def _():
            own_copy(pair).start()

    pl.semaphore_wait(barrier, heights * surfs + 1)
    mate_copy.start()
    for k in range(1, heights):
        g_copy(order(k)).start()
    for n in range(pieces):
        y_copy(n).start()

    load_forward.wait()
    load_panel.wait()
    panel_spectra(0, 0, 0, 0, depth)
    shot_spectra(0)
    for load in load_small:
        load.wait()
    line_row, far, swap, base = [where_ref[n:n + 1, :] for n in range(4)]
    panel = line_row + 2 * (far + side - 2 * side * far) + swap + core - 2 * core * swap
    target = base
    for n in range(4 * heights):
        target = target + jnp.where(panel == n, plan_ref[n], 0)
    place_rows[...] = jnp.where(
        lax.broadcasted_iota(jnp.int32, place_rows.shape, 0) == target, 1.0, 0.0
    ).astype(BF16)
    load_inverse.wait()
    mate_copy.wait_recv()
    panel_spectra(1, 0, 1, 0, depth)

    def take_piece(n):
        pltpu.make_async_copy(panels.at[2, rows_of(n)], panels.at[2, rows_of(n)], y_recv.at[n]).wait()
        relay_copy(n).start()
        panel_spectra(2, 1, 0, n, BLOCK)

    work(0, 0, 0)

    def first_pair(e, carry):
        slot = order(e)
        pltpu.make_async_copy(gathered.at[slot], gathered.at[slot], g_recv.at[slot]).wait()
        shot_spectra(e)
        work(e, e, 0)
        return carry

    def y_piece(n, carry):
        take_piece(n)
        return carry

    first_pair(1, 0)
    y_piece(0, 0)
    lax.fori_loop(2, heights, first_pair, 0)
    lax.fori_loop(1, pieces, y_piece, 0)

    def relayed_piece(n, carry):
        pltpu.make_async_copy(panels.at[3, rows_of(n)], panels.at[3, rows_of(n)], relay_recv.at[n]).wait()
        panel_spectra(3, 1, 1, n, BLOCK)
        return carry

    lax.fori_loop(0, pieces, relayed_piece, 0)

    def second_pair(e, carry):
        work(e, items - 1 - e, 1)
        return carry

    lax.fori_loop(heights, items, second_pair, 0)

    chunk = 2 * surfs * rows_item
    receivers = data_ref.shape[1]
    for k in reversed(range(heights)):
        z = order(k)
        for pair in range(2):
            for h in range(surfs):
                slot = arrived.at[z, pair, h]
                if k:
                    pltpu.make_async_copy(slot, slot, leave_recv.at[z, pair, h]).wait()
                else:

                    @pl.when(h != surf)
                    def _():
                        pltpu.make_async_copy(slot, slot, leave_recv.at[z, pair, h]).wait()

                    @pl.when(h == surf)
                    def _():
                        own_copy(pair).wait()

        part = jnp.dot(
            place_rows[:, pl.ds(pl.multiple_of(z * chunk, chunk), chunk)],
            arrived[z].reshape(chunk, samples),
            preferred_element_type=F32,
        )
        if k == heights - 1:
            prediction[...] = part
        elif k:
            prediction[...] += part
        else:
            for s in range(shots):
                low = s * receivers
                total = prediction[low:low + receivers] + part[low:low + receivers]
                out_ref[s] = data_ref[s] - scale_ref[s] * total

    def settle(z, carry):
        for h in range(surfs):

            @pl.when((z != 0) | (h != surf))
            def _():
                leave_copy(z, h).wait_send()
                leave_copy(items - 1 - z, h).wait_send()

        @pl.when(z != height)
        def _():
            g_copy(z).wait_send()

        return carry

    lax.fori_loop(0, heights, settle, 0)
    for n in range(pieces):
        y_copy(n).wait_send()
        relay_copy(n).wait_send()
    mate_copy.wait_send()


def on_device(heights, surfs, data, positions, plan, primaries, scale):
    shots, receivers, samples = data.shape
    depth, width, _, taps = primaries.shape
    per_surf = width // surfs
    half = -(-(samples + taps - 1) // 256) * 128
    forward, inverse = fourier_matrices(samples, 2 * half)
    rows = shots * 2 * per_surf
    items = 2 * heights
    pieces = depth // BLOCK
    panels = 4 * heights
    order = [
        (4 * z, pair, b, s * receivers + q * panels)
        for z in range(heights)
        for pair in range(2)
        for _ in range(surfs)
        for s in range(shots)
        for b in range(2)
        for q in range(per_surf)
    ]
    where_rows = np.zeros((8, len(order)), np.int32)
    where_rows[:4] = np.array(order, np.int32).T
    anywhere = pl.BlockSpec(memory_space=pl.ANY)
    dma = pltpu.SemaphoreType.DMA
    sizes = (heights, surfs, shots, depth, width, samples, taps, half)
    spectra = pltpu.VMEM((2, half // 128, depth, 2, width, 128), F32)
    return pl.pallas_call(
        functools.partial(predict_kernel, sizes),
        out_shape=pltpu.VMEM(data.shape, F32),
        in_specs=[anywhere] * 8,
        out_specs=pl.BlockSpec(memory_space=pltpu.VMEM),
        scratch_shapes=[
            pltpu.SMEM(plan.shape, jnp.int32),
            pltpu.SMEM(scale.shape, F32),
            pltpu.VMEM(where_rows.shape, jnp.int32),
            pltpu.VMEM((1, receivers), jnp.int32),
            pltpu.VMEM(data.shape, F32),
            pltpu.VMEM(forward.shape, BF16),
            pltpu.VMEM(inverse.shape, BF16),
            pltpu.VMEM((4, depth * width, taps), BF16),
            pltpu.VMEM((heights, shots * depth, samples), BF16),
            spectra,
            spectra,
            spectra,
            pltpu.VMEM((heights, half // 128, shots * 3, depth + 8, 128), F32),
            pltpu.VMEM((surfs * rows, 2 * half), F32),
            pltpu.VMEM((items, surfs, rows, samples), BF16),
            pltpu.VMEM((heights, 2, surfs, rows, samples), BF16),
            pltpu.VMEM((shots * receivers, len(order)), BF16),
            pltpu.VMEM((shots * receivers, samples), F32),
            dma((7,)),
            dma((shots,)),
            dma((2,)),
            dma((pieces,)),
            dma((pieces,)),
            dma((pieces,)),
            dma((pieces,)),
            dma((heights,)),
            dma((heights,)),
            dma((items, surfs)),
            dma((heights, 2, surfs)),
            dma((2,)),
        ],
        compiler_params=pltpu.CompilerParams(
            collective_id=0, has_side_effects=True, vmem_limit_bytes=57000 * 1024
        ),
        name="predict",
    )(
        plan,
        scale,
        jnp.asarray(where_rows),
        positions.reshape(1, receivers),
        data,
        primaries.reshape(depth * width, taps),
        jnp.asarray(forward),
        jnp.asarray(inverse),
    )


def solution(mesh):
    heights, surfs = mesh.shape["shot"] // 4, mesh.shape["surf"]
    in_specs = (P("shot", "surf", None), P("surf"), P(), P("surf", None, "shot", None), P("shot"))
    out_specs = P("shot", "surf", None)
    return jax.shard_map(
        functools.partial(on_device, heights, surfs),
        mesh=mesh, in_specs=in_specs, out_specs=out_specs, check_vma=False,
    )
```

```python
import functools
import math

import jax
import jax.numpy as jnp
import ml_dtypes
import numpy as np
from jax import lax
from jax.experimental import pallas as pl
from jax.experimental.pallas import tpu as pltpu
from jax.sharding import PartitionSpec as P

MESH = pl.DeviceIdType.MESH
F32 = jnp.float32
BF16 = jnp.bfloat16
BLOCK = 16


def fourier_matrices(samples, length):
    half = length // 2
    time, frequency = np.arange(samples), np.arange(half)
    angles = (time[:, None] * frequency[None, :] % length) * (2.0 * math.pi / length)
    cosine, sine = np.cos(angles), np.sin(angles)
    forward_imag = -sine
    forward_imag[:, 0] = 1.0 - 2.0 * (time % 2)
    forward = np.concatenate([cosine, forward_imag], axis=1)
    weights = np.where(frequency == 0, 1.0, 2.0) / length
    weights = np.concatenate([weights, weights])
    inverse = forward.T * weights[:, None]
    return forward.astype(ml_dtypes.bfloat16), inverse.astype(ml_dtypes.bfloat16)


def predict_kernel(
    sizes,
    plan_hbm, scale_hbm, where_hbm, positions_hbm, data_hbm, primaries_hbm, forward_hbm, inverse_hbm,
    out_ref,
    plan_ref, scale_ref, where_ref, positions_ref, data_ref, forward_ref, inverse_ref,
    panels, gathered, e1, e2, e3, factors, spectrum, leaving, arrived, place_rows, prediction,
    load_sems, data_sems, mate_sems, y_send, y_recv, relay_send, relay_recv, g_send, g_recv,
    leave_send, leave_recv, own_sems,
):
    heights, surfs, shots, depth, width, samples, taps, half = sizes
    per_surf = width // surfs
    pieces = depth // BLOCK
    piece_rows = BLOCK * width
    rows_item = shots * 2 * per_surf
    items = 2 * heights
    tiles_f = half // 128
    shot = lax.axis_index("shot")
    surf = lax.axis_index("surf")
    core = shot % 2
    side = shot // 2 % 2
    height = shot // 4
    mate = (height * 2 + side) * 2 + 1 - core

    def across(n):
        return (height * 2 + 1 - side) * 2 + (core + n) % 2

    def line(z):
        return (z * 2 + side) * 2 + core

    barrier = pltpu.get_barrier_semaphore()
    for to in (across(0), across(1), mate):
        pl.semaphore_signal(barrier, inc=1, device_id=(to, surf), device_id_type=MESH)
    for z in range(heights):
        for h in range(surfs):

            @pl.when((z != height) | (h != surf))
            def _():
                pl.semaphore_signal(barrier, inc=1, device_id=(line(z), h), device_id_type=MESH)

    load_positions = pltpu.make_async_copy(positions_hbm, positions_ref, load_sems.at[0])
    load_positions.start()
    load_data = [pltpu.make_async_copy(data_hbm.at[s], data_ref.at[s], data_sems.at[s]) for s in range(shots)]
    for load in load_data:
        load.start()
    load_panel = pltpu.make_async_copy(primaries_hbm, panels.at[0], load_sems.at[1])
    load_forward = pltpu.make_async_copy(forward_hbm, forward_ref, load_sems.at[2])
    load_inverse = pltpu.make_async_copy(inverse_hbm, inverse_ref, load_sems.at[3])
    load_small = [
        pltpu.make_async_copy(src, dst, load_sems.at[4 + n])
        for n, (src, dst) in enumerate(((plan_hbm, plan_ref), (scale_hbm, scale_ref), (where_hbm, where_ref)))
    ]
    mate_copy = pltpu.make_async_remote_copy(
        src_ref=primaries_hbm,
        dst_ref=panels.at[1],
        send_sem=mate_sems.at[0],
        recv_sem=mate_sems.at[1],
        device_id=(mate, surf),
        device_id_type=MESH,
    )

    def rows_of(n):
        return pl.ds(pl.multiple_of(n * piece_rows, piece_rows), piece_rows)

    def y_copy(n):
        return pltpu.make_async_remote_copy(
            src_ref=primaries_hbm.at[rows_of(n)],
            dst_ref=panels.at[2 + n % 2, rows_of(n)],
            send_sem=y_send.at[n],
            recv_sem=y_recv.at[n],
            device_id=(across(n), surf),
            device_id_type=MESH,
        )

    def relay_copy(n):
        return pltpu.make_async_remote_copy(
            src_ref=panels.at[2 + n % 2, rows_of(n)],
            dst_ref=panels.at[3 - n % 2, rows_of(n)],
            send_sem=relay_send.at[n],
            recv_sem=relay_recv.at[n],
            device_id=(mate, surf),
            device_id_type=MESH,
        )

    load_positions.wait()
    local = positions_ref[...] - surf * depth
    onehot = jnp.where(
        lax.broadcasted_iota(jnp.int32, (depth, local.shape[1]), 0) == local, 1.0, 0.0
    ).astype(BF16)
    for s in range(shots):
        load_data[s].wait()
        if s == shots - 1:
            load_panel.start()
            load_forward.start()
            load_inverse.start()
            for load in load_small:
                load.start()
        value = data_ref[s]
        top = value.astype(BF16)
        rest = value - top.astype(F32)
        middle = rest.astype(BF16)
        low = (rest - middle.astype(F32)).astype(BF16)
        total = (
            jnp.dot(onehot, top, preferred_element_type=F32)
            + jnp.dot(onehot, middle, preferred_element_type=F32)
            + jnp.dot(onehot, low, preferred_element_type=F32)
        )
        gathered[height, s * depth:(s + 1) * depth, :] = total.astype(BF16)

    def order(k):
        upper = height // (heights // 2)
        toward = 1 - 2 * upper
        short = height + upper * (heights - 1 - 2 * height)
        past = (k - 2 * short - 1 + 4 * heights) // (4 * heights)
        near = (k + 1) // 2 * (2 * (k % 2) - 1)
        return height + toward * (past * (k - short) + (1 - past) * near)

    def g_copy(z):
        return pltpu.make_async_remote_copy(
            src_ref=gathered.at[height],
            dst_ref=gathered.at[height],
            send_sem=g_send.at[z],
            recv_sem=g_recv.at[height],
            device_id=(line(z), surf),
            device_id_type=MESH,
        )

    def panel_spectra(which, pair, lane, n, block):
        rows = panels[which, pl.ds(pl.multiple_of(n * block * width, block * width), block * width), :]
        value = jnp.dot(rows, forward_ref[:taps, :], preferred_element_type=F32)
        real, imag = value[:, :half], value[:, half:]
        first = lax.broadcasted_iota(jnp.int32, real.shape, 1) == 0
        at = pl.ds(pl.multiple_of(n * block, block), block)
        values = (
            jnp.where(first, 0.0, real),
            jnp.where(first, real, imag - real),
            jnp.where(first, imag, imag + real),
        )
        for ref, value in zip((e1, e2, e3), values):
            for f in range(tiles_f):
                ref[pair, f, at, lane] = value[:, f * 128:(f + 1) * 128].reshape(block, width, 128)

    def place_of(e):
        pair = e // heights
        return pair, e + pair * (items - 1 - 2 * e)

    def leave_copy(e, h):
        pair, k = place_of(e)
        return pltpu.make_async_remote_copy(
            src_ref=leaving.at[e, h],
            dst_ref=arrived.at[height, pair, surf],
            send_sem=leave_send.at[e, h],
            recv_sem=leave_recv.at[height, pair, surf],
            device_id=(line(order(k)), h),
            device_id_type=MESH,
        )

    def own_copy(pair):
        return pltpu.make_async_copy(
            leaving.at[pair * (items - 1), surf], arrived.at[height, pair, surf], own_sems.at[pair]
        )

    def shot_spectra(k):
        slot = order(k)
        value = jnp.dot(gathered[slot], forward_ref[...], preferred_element_type=F32)
        real, imag = value[:, :half], value[:, half:]
        for m, part in enumerate((real + imag, real, imag)):
            for s in range(shots):
                for f in range(tiles_f):
                    factors[k, f, s * 3 + m, :depth, :] = part[
                        s * depth:(s + 1) * depth, f * 128:(f + 1) * 128
                    ]

    def work(e, k, pair):
        tiles = 2 * width // 8
        first = lax.broadcasted_iota(jnp.int32, (2 * width, 128), 1) == 0
        back = None
        for f in range(tiles_f):
            sums = [None] * (3 * shots * tiles)
            for x in range(depth):
                rows = [
                    jnp.broadcast_to(factors[k, f, n, x:x + 1], (8, 128)) for n in range(3 * shots)
                ]
                for t in range(tiles):
                    b, q = t * 8 // width, t * 8 % width
                    for m, ref in enumerate((e1, e2, e3)):
                        factor = ref[pair, f, x, b, q:q + 8]
                        for s in range(shots):
                            at = (s * 3 + m) * tiles + t
                            term = factor * rows[s * 3 + m]
                            sums[at] = term if sums[at] is None else sums[at] + term
            for s in range(shots):
                k1, k2, k3 = [
                    jnp.concatenate(sums[(s * 3 + m) * tiles:(s * 3 + m + 1) * tiles], axis=0)
                    for m in range(3)
                ]
                re, im = k1 - k3, k1 + k2
                if f == 0:
                    re, im = jnp.where(first, k2, re), jnp.where(first, k3, im)
                for h in range(surfs):
                    for b in range(2):
                        low = ((h * shots + s) * 2 + b) * per_surf
                        src = b * width + h * per_surf
                        spectrum[low:low + per_surf, f * 256:f * 256 + 128] = re[src:src + per_surf]
                        spectrum[low:low + per_surf, f * 256 + 128:f * 256 + 256] = im[src:src + per_surf]
            lanes = slice(f * 256, f * 256 + 256)
            part = jnp.dot(spectrum[:, lanes].astype(BF16), inverse_ref[lanes, :], preferred_element_type=F32)
            back = part if back is None else back + part
        for h in range(surfs):
            leaving[e, h] = back[h * rows_item:(h + 1) * rows_item].astype(BF16)
        for h in range(surfs):

            @pl.when((k != 0) | (h != surf))
            def _():
                leave_copy(e, h).start()

        @pl.when(k == 0)
        def _():
            own_copy(pair).start()

    pl.semaphore_wait(barrier, heights * surfs + 2)
    mate_copy.start()
    for k in range(1, heights):
        g_copy(order(k)).start()
    for n in range(pieces):
        y_copy(n).start()

    load_forward.wait()
    load_panel.wait()
    panel_spectra(0, 0, 0, 0, depth)
    shot_spectra(0)
    for load in load_small:
        load.wait()
    line_row, far, swap, base = [where_ref[n:n + 1, :] for n in range(4)]
    panel = line_row + 2 * (far + side - 2 * side * far) + swap + core - 2 * core * swap
    target = base
    for n in range(4 * heights):
        target = target + jnp.where(panel == n, plan_ref[n], 0)
    place_rows[...] = jnp.where(
        lax.broadcasted_iota(jnp.int32, place_rows.shape, 0) == target, 1.0, 0.0
    ).astype(BF16)
    load_inverse.wait()
    mate_copy.wait_recv()
    panel_spectra(1, 0, 1, 0, depth)

    def take_piece(n):
        piece = panels.at[2 + n % 2, rows_of(n)]
        pltpu.make_async_copy(piece, piece, y_recv.at[n]).wait()
        relay_copy(n).start()
        panel_spectra(2 + n % 2, 1, n % 2, n, BLOCK)

    work(0, 0, 0)

    def first_pair(e, carry):
        slot = order(e)
        pltpu.make_async_copy(gathered.at[slot], gathered.at[slot], g_recv.at[slot]).wait()
        shot_spectra(e)
        work(e, e, 0)
        return carry

    def y_piece(n, carry):
        take_piece(n)
        return carry

    first_pair(1, 0)
    y_piece(0, 0)
    lax.fori_loop(2, heights, first_pair, 0)
    lax.fori_loop(1, pieces, y_piece, 0)

    def relayed_piece(n, carry):
        piece = panels.at[3 - n % 2, rows_of(n)]
        pltpu.make_async_copy(piece, piece, relay_recv.at[n]).wait()
        panel_spectra(3 - n % 2, 1, 1 - n % 2, n, BLOCK)
        return carry

    lax.fori_loop(0, pieces, relayed_piece, 0)

    def second_pair(e, carry):
        work(e, items - 1 - e, 1)
        return carry

    lax.fori_loop(heights, items, second_pair, 0)

    chunk = 2 * surfs * rows_item
    receivers = data_ref.shape[1]
    for k in reversed(range(heights)):
        z = order(k)
        for pair in range(2):
            for h in range(surfs):
                slot = arrived.at[z, pair, h]
                if k:
                    pltpu.make_async_copy(slot, slot, leave_recv.at[z, pair, h]).wait()
                else:

                    @pl.when(h != surf)
                    def _():
                        pltpu.make_async_copy(slot, slot, leave_recv.at[z, pair, h]).wait()

                    @pl.when(h == surf)
                    def _():
                        own_copy(pair).wait()

        part = jnp.dot(
            place_rows[:, pl.ds(pl.multiple_of(z * chunk, chunk), chunk)],
            arrived[z].reshape(chunk, samples),
            preferred_element_type=F32,
        )
        if k == heights - 1:
            prediction[...] = part
        elif k:
            prediction[...] += part
        else:
            for s in range(shots):
                low = s * receivers
                total = prediction[low:low + receivers] + part[low:low + receivers]
                out_ref[s] = data_ref[s] - scale_ref[s] * total

    def settle(z, carry):
        for h in range(surfs):

            @pl.when((z != 0) | (h != surf))
            def _():
                leave_copy(z, h).wait_send()
                leave_copy(items - 1 - z, h).wait_send()

        @pl.when(z != height)
        def _():
            g_copy(z).wait_send()

        return carry

    lax.fori_loop(0, heights, settle, 0)
    for n in range(pieces):
        y_copy(n).wait_send()
        relay_copy(n).wait_send()
    mate_copy.wait_send()


def on_device(heights, surfs, data, positions, plan, primaries, scale):
    shots, receivers, samples = data.shape
    depth, width, _, taps = primaries.shape
    per_surf = width // surfs
    half = -(-(samples + taps - 1) // 256) * 128
    forward, inverse = fourier_matrices(samples, 2 * half)
    inverse = inverse.reshape(2, half // 128, 128, samples).transpose(1, 0, 2, 3).reshape(inverse.shape)
    rows = shots * 2 * per_surf
    items = 2 * heights
    pieces = depth // BLOCK
    panels = 4 * heights
    order = [
        (4 * z, pair, b, s * receivers + q * panels)
        for z in range(heights)
        for pair in range(2)
        for _ in range(surfs)
        for s in range(shots)
        for b in range(2)
        for q in range(per_surf)
    ]
    where_rows = np.zeros((8, len(order)), np.int32)
    where_rows[:4] = np.array(order, np.int32).T
    anywhere = pl.BlockSpec(memory_space=pl.ANY)
    dma = pltpu.SemaphoreType.DMA
    sizes = (heights, surfs, shots, depth, width, samples, taps, half)
    spectra = pltpu.VMEM((2, half // 128, depth, 2, width, 128), F32)
    return pl.pallas_call(
        functools.partial(predict_kernel, sizes),
        out_shape=pltpu.VMEM(data.shape, F32),
        in_specs=[anywhere] * 8,
        out_specs=pl.BlockSpec(memory_space=pltpu.VMEM),
        scratch_shapes=[
            pltpu.SMEM(plan.shape, jnp.int32),
            pltpu.SMEM(scale.shape, F32),
            pltpu.VMEM(where_rows.shape, jnp.int32),
            pltpu.VMEM((1, receivers), jnp.int32),
            pltpu.VMEM(data.shape, F32),
            pltpu.VMEM(forward.shape, BF16),
            pltpu.VMEM(inverse.shape, BF16),
            pltpu.VMEM((4, depth * width, taps), BF16),
            pltpu.VMEM((heights, shots * depth, samples), BF16),
            spectra,
            spectra,
            spectra,
            pltpu.VMEM((heights, half // 128, shots * 3, depth + 8, 128), F32),
            pltpu.VMEM((surfs * rows, 2 * half), F32),
            pltpu.VMEM((items, surfs, rows, samples), BF16),
            pltpu.VMEM((heights, 2, surfs, rows, samples), BF16),
            pltpu.VMEM((shots * receivers, len(order)), BF16),
            pltpu.VMEM((shots * receivers, samples), F32),
            dma((7,)),
            dma((shots,)),
            dma((2,)),
            dma((pieces,)),
            dma((pieces,)),
            dma((pieces,)),
            dma((pieces,)),
            dma((heights,)),
            dma((heights,)),
            dma((items, surfs)),
            dma((heights, 2, surfs)),
            dma((2,)),
        ],
        compiler_params=pltpu.CompilerParams(
            collective_id=0, has_side_effects=True, vmem_limit_bytes=57000 * 1024
        ),
        name="predict",
    )(
        plan,
        scale,
        jnp.asarray(where_rows),
        positions.reshape(1, receivers),
        data,
        primaries.reshape(depth * width, taps),
        jnp.asarray(forward),
        jnp.asarray(inverse),
    )


def solution(mesh):
    heights, surfs = mesh.shape["shot"] // 4, mesh.shape["surf"]
    in_specs = (P("shot", "surf", None), P("surf"), P(), P("surf", None, "shot", None), P("shot"))
    out_specs = P("shot", "surf", None)
    return jax.shard_map(
        functools.partial(on_device, heights, surfs),
        mesh=mesh, in_specs=in_specs, out_specs=out_specs, check_vma=False,
    )
```

```python
import functools
import math

import jax
import jax.numpy as jnp
import ml_dtypes
import numpy as np
from jax import lax
from jax.experimental import pallas as pl
from jax.experimental.pallas import tpu as pltpu
from jax.sharding import PartitionSpec as P

MESH = pl.DeviceIdType.MESH
F32 = jnp.float32
BF16 = jnp.bfloat16
UNROLL = 32
BLOCK = 16


def fourier_matrices(samples, length):
    half = length // 2
    time, frequency = np.arange(samples), np.arange(half)
    angles = (time[:, None] * frequency[None, :] % length) * (2.0 * math.pi / length)
    cosine, sine = np.cos(angles), np.sin(angles)
    forward_imag = -sine
    forward_imag[:, 0] = 1.0 - 2.0 * (time % 2)
    forward = np.concatenate([cosine, forward_imag], axis=1)
    weights = np.where(frequency == 0, 1.0, 2.0) / length
    weights = np.concatenate([weights, weights])
    inverse = forward.T * weights[:, None]
    return forward.astype(ml_dtypes.bfloat16), inverse.astype(ml_dtypes.bfloat16)


def predict_kernel(
    sizes,
    plan_hbm, scale_hbm, where_hbm, positions_hbm, data_hbm, primaries_hbm, forward_hbm, inverse_hbm,
    out_ref,
    plan_ref, scale_ref, where_ref, positions_ref, data_ref, forward_ref, inverse_ref,
    panels, gathered, e1, e2, e3, factors, spectrum, leaving, arrived, place_rows, prediction,
    load_sems, data_sems, mate_sems, y_send, y_recv, relay_send, relay_recv, g_send, g_recv,
    leave_send, leave_recv, own_sems,
):
    heights, surfs, shots, depth, width, samples, taps, half = sizes
    per_surf = width // surfs
    pieces = depth // BLOCK
    piece_rows = BLOCK * width
    rows_item = shots * 2 * per_surf
    items = 2 * heights
    tiles_f = half // 128
    shot = lax.axis_index("shot")
    surf = lax.axis_index("surf")
    core = shot % 2
    side = shot // 2 % 2
    height = shot // 4
    mate = (height * 2 + side) * 2 + 1 - core
    across = (height * 2 + 1 - side) * 2 + core

    def line(z):
        return (z * 2 + side) * 2 + core

    barrier = pltpu.get_barrier_semaphore()
    for to in (across, mate):
        pl.semaphore_signal(barrier, inc=1, device_id=(to, surf), device_id_type=MESH)
    for z in range(heights):
        for h in range(surfs):

            @pl.when((z != height) | (h != surf))
            def _():
                pl.semaphore_signal(barrier, inc=1, device_id=(line(z), h), device_id_type=MESH)

    load_positions = pltpu.make_async_copy(positions_hbm, positions_ref, load_sems.at[0])
    load_positions.start()
    load_data = [pltpu.make_async_copy(data_hbm.at[s], data_ref.at[s], data_sems.at[s]) for s in range(shots)]
    for load in load_data:
        load.start()
    load_panel = pltpu.make_async_copy(primaries_hbm, panels.at[0], load_sems.at[1])
    load_forward = pltpu.make_async_copy(forward_hbm, forward_ref, load_sems.at[2])
    load_inverse = pltpu.make_async_copy(inverse_hbm, inverse_ref, load_sems.at[3])
    load_small = [
        pltpu.make_async_copy(src, dst, load_sems.at[4 + n])
        for n, (src, dst) in enumerate(((plan_hbm, plan_ref), (scale_hbm, scale_ref), (where_hbm, where_ref)))
    ]
    mate_copy = pltpu.make_async_remote_copy(
        src_ref=primaries_hbm,
        dst_ref=panels.at[1],
        send_sem=mate_sems.at[0],
        recv_sem=mate_sems.at[1],
        device_id=(mate, surf),
        device_id_type=MESH,
    )

    def rows_of(n):
        return pl.ds(pl.multiple_of(n * piece_rows, piece_rows), piece_rows)

    def y_copy(n):
        return pltpu.make_async_remote_copy(
            src_ref=primaries_hbm.at[rows_of(n)],
            dst_ref=panels.at[2, rows_of(n)],
            send_sem=y_send.at[n],
            recv_sem=y_recv.at[n],
            device_id=(across, surf),
            device_id_type=MESH,
        )

    def relay_copy(n):
        return pltpu.make_async_remote_copy(
            src_ref=panels.at[2, rows_of(n)],
            dst_ref=panels.at[3, rows_of(n)],
            send_sem=relay_send.at[n],
            recv_sem=relay_recv.at[n],
            device_id=(mate, surf),
            device_id_type=MESH,
        )

    load_positions.wait()
    local = positions_ref[...] - surf * depth
    onehot = jnp.where(
        lax.broadcasted_iota(jnp.int32, (depth, local.shape[1]), 0) == local, 1.0, 0.0
    ).astype(BF16)
    for s in range(shots):
        load_data[s].wait()
        if s == shots - 1:
            load_panel.start()
            load_forward.start()
            load_inverse.start()
            for load in load_small:
                load.start()
        value = data_ref[s]
        top = value.astype(BF16)
        rest = value - top.astype(F32)
        middle = rest.astype(BF16)
        low = (rest - middle.astype(F32)).astype(BF16)
        total = (
            jnp.dot(onehot, top, preferred_element_type=F32)
            + jnp.dot(onehot, middle, preferred_element_type=F32)
            + jnp.dot(onehot, low, preferred_element_type=F32)
        )
        gathered[height, s * depth:(s + 1) * depth, :] = total.astype(BF16)

    def order(k):
        upper = height // (heights // 2)
        toward = 1 - 2 * upper
        short = height + upper * (heights - 1 - 2 * height)
        past = (k - 2 * short - 1 + 4 * heights) // (4 * heights)
        near = (k + 1) // 2 * (2 * (k % 2) - 1)
        return height + toward * (past * (k - short) + (1 - past) * near)

    def g_copy(z):
        return pltpu.make_async_remote_copy(
            src_ref=gathered.at[height],
            dst_ref=gathered.at[height],
            send_sem=g_send.at[z],
            recv_sem=g_recv.at[height],
            device_id=(line(z), surf),
            device_id_type=MESH,
        )

    def panel_spectra(which, pair, lane, n, block):
        rows = panels[which, pl.ds(pl.multiple_of(n * block * width, block * width), block * width), :]
        value = jnp.dot(rows, forward_ref[:taps, :], preferred_element_type=F32)
        real, imag = value[:, :half], value[:, half:]
        first = lax.broadcasted_iota(jnp.int32, real.shape, 1) == 0
        at = pl.ds(pl.multiple_of(n * block, block), block)
        values = (
            jnp.where(first, 0.0, real),
            jnp.where(first, real, imag - real),
            jnp.where(first, imag, imag + real),
        )
        for ref, value in zip((e1, e2, e3), values):
            for f in range(tiles_f):
                ref[pair, f, at, lane] = value[:, f * 128:(f + 1) * 128].reshape(block, width, 128)

    def place_of(e):
        pair = e // heights
        return pair, e + pair * (items - 1 - 2 * e)

    def leave_copy(e, h):
        pair, k = place_of(e)
        return pltpu.make_async_remote_copy(
            src_ref=leaving.at[e, h],
            dst_ref=arrived.at[height, pair, surf],
            send_sem=leave_send.at[e, h],
            recv_sem=leave_recv.at[height, pair, surf],
            device_id=(line(order(k)), h),
            device_id_type=MESH,
        )

    def own_copy(pair):
        return pltpu.make_async_copy(
            leaving.at[pair * (items - 1), surf], arrived.at[height, pair, surf], own_sems.at[pair]
        )

    def shot_spectra(k):
        slot = order(k)
        value = jnp.dot(gathered[slot], forward_ref[...], preferred_element_type=F32)
        real, imag = value[:, :half], value[:, half:]
        for m, part in enumerate((real + imag, real, imag)):
            for s in range(shots):
                for f in range(tiles_f):
                    factors[k, f, s * 3 + m, :depth, :] = part[
                        s * depth:(s + 1) * depth, f * 128:(f + 1) * 128
                    ]

    def work(e, k, pair):
        def one_tile(f, inner):
            lanes = pl.ds(pl.multiple_of(f * 128, 128), 128)
            tiles = 2 * width // 8

            def positions(n, sums):
                sums = list(sums)
                for j in range(UNROLL):
                    x = n * UNROLL + j
                    rows = [
                        [
                            jnp.broadcast_to(
                                factors.at[k, f, s * 3 + m, pl.ds(pl.multiple_of(n * UNROLL, UNROLL), UNROLL)][j:j + 1],
                                (8, 128),
                            )
                            for m in range(3)
                        ]
                        for s in range(shots)
                    ]
                    for t in range(tiles):
                        b, q = t * 8 // width, t * 8 % width
                        for m, ref in enumerate((e1, e2, e3)):
                            factor = ref[pair, f, x, b, q:q + 8]
                            for s in range(shots):
                                at = (s * 3 + m) * tiles + t
                                sums[at] = sums[at] + factor * rows[s][m]
                return tuple(sums)

            zero = jnp.zeros((8, 128), F32)
            sums = lax.fori_loop(
                0, depth // UNROLL, positions, (zero,) * (3 * shots * tiles)
            )
            k1, k2, k3 = [
                [
                    jnp.concatenate(sums[(s * 3 + m) * tiles:(s * 3 + m + 1) * tiles], axis=0)
                    for s in range(shots)
                ]
                for m in range(3)
            ]
            first = lax.broadcasted_iota(jnp.int32, (2 * width, 128), 1) + f * 128 == 0
            imag_lanes = pl.ds(pl.multiple_of(half + f * 128, 128), 128)
            for s in range(shots):
                re = jnp.where(first, k2[s], k1[s] - k3[s])
                im = jnp.where(first, k3[s], k1[s] + k2[s])
                for h in range(surfs):
                    for b in range(2):
                        low = ((h * shots + s) * 2 + b) * per_surf
                        src = b * width + h * per_surf
                        spectrum[low:low + per_surf, lanes] = re[src:src + per_surf]
                        spectrum[low:low + per_surf, imag_lanes] = im[src:src + per_surf]
            return inner

        lax.fori_loop(0, tiles_f, one_tile, 0)
        back = jnp.dot(spectrum[...].astype(BF16), inverse_ref[...], preferred_element_type=F32)
        rows = shots * 2 * per_surf
        for h in range(surfs):
            leaving[e, h] = back[h * rows:(h + 1) * rows].astype(BF16)
        for h in range(surfs):

            @pl.when((k != 0) | (h != surf))
            def _():
                leave_copy(e, h).start()

        @pl.when(k == 0)
        def _():
            own_copy(pair).start()

    pl.semaphore_wait(barrier, heights * surfs + 1)
    mate_copy.start()
    for k in range(1, heights):
        g_copy(order(k)).start()
    for n in range(pieces):
        y_copy(n).start()

    load_forward.wait()
    load_panel.wait()
    panel_spectra(0, 0, 0, 0, depth)
    shot_spectra(0)
    for load in load_small:
        load.wait()
    line_row, far, swap, base = [where_ref[n:n + 1, :] for n in range(4)]
    panel = line_row + 2 * (far + side - 2 * side * far) + swap + core - 2 * core * swap
    target = base
    for n in range(4 * heights):
        target = target + jnp.where(panel == n, plan_ref[n], 0)
    place_rows[...] = jnp.where(
        lax.broadcasted_iota(jnp.int32, place_rows.shape, 0) == target, 1.0, 0.0
    ).astype(BF16)
    load_inverse.wait()
    mate_copy.wait_recv()
    panel_spectra(1, 0, 1, 0, depth)

    def take_piece(n):
        pltpu.make_async_copy(panels.at[2, rows_of(n)], panels.at[2, rows_of(n)], y_recv.at[n]).wait()
        relay_copy(n).start()
        panel_spectra(2, 1, 0, n, BLOCK)

    work(0, 0, 0)

    def first_pair(e, carry):
        slot = order(e)
        pltpu.make_async_copy(gathered.at[slot], gathered.at[slot], g_recv.at[slot]).wait()
        shot_spectra(e)
        work(e, e, 0)
        return carry

    def y_piece(n, carry):
        take_piece(n)
        return carry

    first_pair(1, 0)
    y_piece(0, 0)
    lax.fori_loop(2, heights, first_pair, 0)
    lax.fori_loop(1, pieces, y_piece, 0)

    def relayed_piece(n, carry):
        pltpu.make_async_copy(panels.at[3, rows_of(n)], panels.at[3, rows_of(n)], relay_recv.at[n]).wait()
        panel_spectra(3, 1, 1, n, BLOCK)
        return carry

    lax.fori_loop(0, pieces, relayed_piece, 0)

    def second_pair(e, carry):
        work(e, items - 1 - e, 1)
        return carry

    lax.fori_loop(heights, items, second_pair, 0)

    chunk = 2 * surfs * rows_item
    receivers = data_ref.shape[1]
    for k in reversed(range(heights)):
        z = order(k)
        for pair in range(2):
            for h in range(surfs):
                slot = arrived.at[z, pair, h]
                if k:
                    pltpu.make_async_copy(slot, slot, leave_recv.at[z, pair, h]).wait()
                else:

                    @pl.when(h != surf)
                    def _():
                        pltpu.make_async_copy(slot, slot, leave_recv.at[z, pair, h]).wait()

                    @pl.when(h == surf)
                    def _():
                        own_copy(pair).wait()

        part = jnp.dot(
            place_rows[:, pl.ds(pl.multiple_of(z * chunk, chunk), chunk)],
            arrived[z].reshape(chunk, samples),
            preferred_element_type=F32,
        )
        if k == heights - 1:
            prediction[...] = part
        elif k:
            prediction[...] += part
        else:
            for s in range(shots):
                low = s * receivers
                total = prediction[low:low + receivers] + part[low:low + receivers]
                out_ref[s] = data_ref[s] - scale_ref[s] * total

    def settle(z, carry):
        for h in range(surfs):

            @pl.when((z != 0) | (h != surf))
            def _():
                leave_copy(z, h).wait_send()
                leave_copy(items - 1 - z, h).wait_send()

        @pl.when(z != height)
        def _():
            g_copy(z).wait_send()

        return carry

    lax.fori_loop(0, heights, settle, 0)
    for n in range(pieces):
        y_copy(n).wait_send()
        relay_copy(n).wait_send()
    mate_copy.wait_send()


def on_device(heights, surfs, data, positions, plan, primaries, scale):
    shots, receivers, samples = data.shape
    depth, width, _, taps = primaries.shape
    per_surf = width // surfs
    half = -(-(samples + taps - 1) // 256) * 128
    forward, inverse = fourier_matrices(samples, 2 * half)
    rows = shots * 2 * per_surf
    items = 2 * heights
    pieces = depth // BLOCK
    panels = 4 * heights
    order = [
        (4 * z, pair, b, s * receivers + q * panels)
        for z in range(heights)
        for pair in range(2)
        for _ in range(surfs)
        for s in range(shots)
        for b in range(2)
        for q in range(per_surf)
    ]
    where_rows = np.zeros((8, len(order)), np.int32)
    where_rows[:4] = np.array(order, np.int32).T
    anywhere = pl.BlockSpec(memory_space=pl.ANY)
    dma = pltpu.SemaphoreType.DMA
    sizes = (heights, surfs, shots, depth, width, samples, taps, half)
    spectra = pltpu.VMEM((2, half // 128, depth, 2, width, 128), F32)
    return pl.pallas_call(
        functools.partial(predict_kernel, sizes),
        out_shape=pltpu.VMEM(data.shape, F32),
        in_specs=[anywhere] * 8,
        out_specs=pl.BlockSpec(memory_space=pltpu.VMEM),
        scratch_shapes=[
            pltpu.SMEM(plan.shape, jnp.int32),
            pltpu.SMEM(scale.shape, F32),
            pltpu.VMEM(where_rows.shape, jnp.int32),
            pltpu.VMEM((1, receivers), jnp.int32),
            pltpu.VMEM(data.shape, F32),
            pltpu.VMEM(forward.shape, BF16),
            pltpu.VMEM(inverse.shape, BF16),
            pltpu.VMEM((4, depth * width, taps), BF16),
            pltpu.VMEM((heights, shots * depth, samples), BF16),
            spectra,
            spectra,
            spectra,
            pltpu.VMEM((heights, half // 128, shots * 3, depth + 8, 128), F32),
            pltpu.VMEM((surfs * rows, 2 * half), F32),
            pltpu.VMEM((items, surfs, rows, samples), BF16),
            pltpu.VMEM((heights, 2, surfs, rows, samples), BF16),
            pltpu.VMEM((shots * receivers, len(order)), BF16),
            pltpu.VMEM((shots * receivers, samples), F32),
            dma((7,)),
            dma((shots,)),
            dma((2,)),
            dma((pieces,)),
            dma((pieces,)),
            dma((pieces,)),
            dma((pieces,)),
            dma((heights,)),
            dma((heights,)),
            dma((items, surfs)),
            dma((heights, 2, surfs)),
            dma((2,)),
        ],
        compiler_params=pltpu.CompilerParams(
            collective_id=0, has_side_effects=True, vmem_limit_bytes=57000 * 1024
        ),
        name="predict",
    )(
        plan,
        scale,
        jnp.asarray(where_rows),
        positions.reshape(1, receivers),
        data,
        primaries.reshape(depth * width, taps),
        jnp.asarray(forward),
        jnp.asarray(inverse),
    )


def solution(mesh):
    heights, surfs = mesh.shape["shot"] // 4, mesh.shape["surf"]
    in_specs = (P("shot", "surf", None), P("surf"), P(), P("surf", None, "shot", None), P("shot"))
    out_specs = P("shot", "surf", None)
    return jax.shard_map(
        functools.partial(on_device, heights, surfs),
        mesh=mesh, in_specs=in_specs, out_specs=out_specs, check_vma=False,
    )
```
